128 devices in a mesh: row: 16 (over z, y), col: 8 (over x, core).
Axes of the slice: x: 4, y: 4, z: 4, core: 2. Of those that a mesh axis runs over, the one named last changes fastest.
Arguments:
- trailing: float32 [16384, 16384], P('row', 'col'), may hold values from -40 to 40, as said below
- factor_one: float32 [16384, 512], P(('row', 'col')), may hold values from -0.0390625 to 0.0390625
- inverse_one: float32 [512, 512], replicated, may hold values from -1 to 2, as said below
- factor_two_top: float32 [512, 512], replicated, may hold values from -0.0390625 to 0.0390625
- factor_two: float32 [16384, 512], P(('row', 'col')), may hold values from -0.0390625 to 0.0390625
- inverse_two: float32 [512, 512], replicated, may hold values from -1 to 2, as said below
- structure_one: int32 [96], replicated, may hold values from 0 to 127, as said below
- structure_two: int32 [94], replicated, may hold values from 0 to 127, as said below
Outputs:
- column_one: float32 [16384, 512], P(('row', 'col'))
- diagonal_one: float32 [512, 512], replicated
- column_two: float32 [16384, 512], P(('row', 'col'))
- cross_two: float32 [512, 512], replicated
- diagonal_two: float32 [512, 512], replicated
The draws below stay inside these ranges and needn't reach their ends.
Inputs may be any that keep to these rules, and one draw needn't show every extreme that they name: `trailing`: symmetric. `inverse_one`: lower triangular, diagonal between 1 and 2. `inverse_two`: lower triangular, diagonal between 1 and 2. `structure_one`: distinct, rising; lists block 0 and the last block. `structure_two`: distinct, rising, each also listed in structure_one; lists block 0 and the last block.
All inputs are finite; a program needn't handle non-finite values.
Results may differ from the reference program's by a relative error of at most 0.0003.
Values sent between devices are 32-bit elements; how exact they have to be, the bound alone decides.
No kernel may reach another device: no remote copies, remote signals or barrier semaphores. Data moves between devices by JAX's collectives and lax.ppermute only.
A program may use at most 128 MiB of HBM per device.

```python
import math
import jax
import jax.numpy as jnp
from jax import lax

W = 512
BLK = 128
M = 16384
SB1 = 96
SB2 = 94


def draw_trailing(key, part):
    normals = jax.random.truncated_normal(jax.random.fold_in(key, 31), -5.0, 5.0, (M, M), jnp.float32)
    symmetric = (normals + normals.T) * 0.7071067811865476
    places = jnp.arange(M, dtype=jnp.int32)
    return symmetric.at[places, places].add(2.0)


def lower_inverse(key):
    diag_values = jax.random.uniform(jax.random.fold_in(key, 1), (W,), jnp.float32, 1.0, 2.0)
    off_diag = jax.random.truncated_normal(jax.random.fold_in(key, 2), -5.0, 5.0, (W, W), jnp.float32) * (0.8 / math.sqrt(W))
    return jnp.tril(off_diag, -1) + jnp.diag(diag_values)


def draw_inverse_one(key, part):
    return lower_inverse(jax.random.fold_in(key, 11))


def draw_inverse_two(key, part):
    return lower_inverse(jax.random.fold_in(key, 12))


def structure_lists(key):
    count = M // BLK
    inner_blocks = jax.random.permutation(jax.random.fold_in(key, 21), count - 2)[:SB1 - 2].astype(jnp.int32) + 1
    ends = jnp.array([0, count - 1], dtype=jnp.int32)
    first_set = jnp.sort(jnp.concatenate([ends, inner_blocks]))
    chosen = jax.random.permutation(jax.random.fold_in(key, 22), SB1 - 2)[:SB2 - 2]
    second_set = jnp.sort(jnp.concatenate([ends, first_set[1:-1][chosen]]))
    return (first_set, second_set)


def draw_structure_one(key, part):
    return structure_lists(key)[0]


def draw_structure_two(key, part):
    return structure_lists(key)[1]


def shard_levels(key, dims, split, smallest, top_value):
    def one(dim, blocks):
        steps = jax.random.uniform(jax.random.fold_in(jax.random.fold_in(key, 6), dim), (blocks,), jnp.float32, smallest / len(split), top_value / len(split))
        return jnp.repeat(jnp.exp(steps), dims[dim] // blocks).reshape((-1,) + (1,) * (len(dims) - dim - 1))

    level = one(*split[0])
    for cut in split[1:]:
        level = level * one(*cut)
    return level


def centred(own_key, shape, deviation, bound, cuts=(), held_as=jnp.bfloat16):
    drawn = jax.random.normal(own_key, shape, jnp.float32) * deviation
    if len(cuts) > 0:
        drawn = shard_levels(own_key, shape, cuts, -0.22, 0.18) * drawn
    return jnp.clip(drawn, min=-bound, max=bound).astype(held_as)


def setup_inputs(seed: int = 0) -> dict:
    splits = jax.random.split(jax.random.key(seed), 9)
    trailing = draw_trailing(jax.random.fold_in(splits[8], 71), 0)
    factor_one = centred(splits[1], (M, W), (2 * SB1 * BLK) ** -0.5, 0.0390625, ((0, 128),), jnp.float32)
    inverse_one = draw_inverse_one(jax.random.fold_in(splits[8], 71), 0)
    factor_two_top = centred(splits[3], (W, W), (2 * (SB2 * BLK + W)) ** -0.5, 0.0390625, (), jnp.float32)
    factor_two = centred(splits[4], (M, W), (2 * (SB2 * BLK + W)) ** -0.5, 0.0390625, ((0, 128),), jnp.float32)
    inverse_two = draw_inverse_two(jax.random.fold_in(splits[8], 71), 0)
    structure_one = draw_structure_one(jax.random.fold_in(splits[8], 71), 0)
    structure_two = draw_structure_two(jax.random.fold_in(splits[8], 71), 0)
    return {"trailing": trailing, "factor_one": factor_one, "inverse_one": inverse_one, "factor_two_top": factor_two_top, "factor_two": factor_two, "inverse_two": inverse_two, "structure_one": structure_one, "structure_two": structure_two}


def product(left, right):
    return jnp.dot(left, right, precision=lax.Precision.HIGHEST, preferred_element_type=jnp.float32)


def block_flags(structure, count):
    blocks = jnp.arange(count, dtype=jnp.int32) // BLK
    hits = jnp.any(blocks[:, None] == structure[None, :].astype(jnp.int32), axis=1)
    return hits.astype(jnp.float32)[:, None]


def reference(trailing, factor_one, inverse_one, factor_two_top, factor_two, inverse_two, structure_one, structure_two):
    mask_one = block_flags(structure_one, M)
    mask_two = block_flags(structure_two, M)
    normal_one = mask_one * product(factor_one, inverse_one)
    column_one = -mask_one * product(trailing, normal_one)
    diagonal_one = product(inverse_one.T, inverse_one) - product(normal_one.T, column_one)
    normal_top = product(factor_two_top, inverse_two)
    normal_two = mask_two * product(factor_two, inverse_two)
    column_two = -mask_two * (product(column_one, normal_top) + product(trailing, normal_two))
    cross_two = -(product(diagonal_one, normal_top) + product(column_one.T, normal_two))
    diagonal_two = product(inverse_two.T, inverse_two) - product(normal_top.T, cross_two) - product(normal_two.T, column_two)
    return column_one, diagonal_one, column_two, cross_two, diagonal_two
```

```python
import functools

import jax
import jax.numpy as jnp
from jax import lax
from jax.experimental import pallas as pl
from jax.experimental.pallas import tpu as pltpu
from jax.sharding import PartitionSpec as P

BLK = 128
W = 512
BOTH = ("row", "col")
SWAP = [(i, i ^ 1) for i in range(8)]
F32 = jnp.float32
BF16 = jnp.bfloat16


def product(left, right):
    return jnp.dot(left, right, precision=lax.Precision.HIGH, preferred_element_type=F32)


def product_t(left, right):
    return lax.dot_general(
        left, right, (((0,), (0,)), ((), ())), precision=lax.Precision.HIGH, preferred_element_type=F32
    )


def block_flag(structure, block):
    return jnp.any(structure == block).astype(F32)


def params():
    return pltpu.CompilerParams(vmem_limit_bytes=48 << 20)


def halves(value):
    high = value.astype(BF16)
    return high, (value - high.astype(F32)).astype(BF16)


def three(left_high, left_low, right_high, right_low):
    dot = functools.partial(jnp.dot, preferred_element_type=F32)
    return dot(left_high, right_high) + (dot(left_low, right_high) + dot(left_high, right_low))


def flip_kernel(block, high, low):
    high[...], low[...] = halves(block[...].T)


def flipped(trailing):
    rows, cols = trailing.shape
    step = 256
    out = jax.ShapeDtypeStruct((cols, rows), BF16)
    spec = pl.BlockSpec((step, rows), lambda i: (i, 0))
    return pl.pallas_call(
        flip_kernel,
        grid=(cols // step,),
        in_specs=[pl.BlockSpec((rows, step), lambda i: (0, i))],
        out_specs=[spec, spec],
        out_shape=[out, out],
        compiler_params=params(),
        name="flip",
    )(trailing)


def far_kernel(rows, places, *refs):
    pieces, flips, outs = refs[:8], refs[8:16], refs[16:]
    high, low, top, bottom = outs
    for i, piece in enumerate(pieces):
        at = pl.ds(pl.multiple_of(places[i] * BLK, BLK), BLK)
        high[at, :], low[at, :] = halves(piece[...])
    panel_high, panel_low = high[...], low[...]
    for half, out in ((0, top), (1, bottom)):
        left_high = jnp.concatenate([flips[4 * 0 + 2 * half][...], flips[4 * 0 + 2 * half + 1][...]], axis=0)
        left_low = jnp.concatenate([flips[4 + 2 * half][...], flips[4 + 2 * half + 1][...]], axis=0)
        out[...] = three(left_high, left_low, panel_high, panel_low)


def far_product(rows, places, pieces, flip_high, flip_low):
    count = flip_high.shape[1]
    whole = lambda shape: pl.BlockSpec(shape, lambda i, r, p: (0, 0))
    block = [pl.BlockSpec((BLK, count), functools.partial(lambda j, i, r, p: (r[j], 0), j)) for j in range(4)]
    return pl.pallas_call(
        far_kernel,
        grid_spec=pltpu.PrefetchScalarGridSpec(
            num_scalar_prefetch=2,
            grid=(1,),
            in_specs=[whole((BLK, W))] * 8 + block + block,
            out_specs=[whole((count, W))] * 2 + [whole((2 * BLK, W))] * 2,
        ),
        out_shape=[jax.ShapeDtypeStruct((count, W), BF16)] * 2 + [jax.ShapeDtypeStruct((2 * BLK, W), F32)] * 2,
        compiler_params=params(),
        name="far",
    )(rows, places, *pieces, *([flip_high] * 4), *([flip_low] * 4))


def near_kernel(rows, *refs):
    flips, (high, low, out) = refs[:8], refs[8:]
    left_high = jnp.concatenate([f[...] for f in flips[:4]], axis=0)
    left_low = jnp.concatenate([f[...] for f in flips[4:]], axis=0)
    out[0] = three(left_high, left_low, high[...], low[...])


def near_product(rows, panel_high, panel_low, flip_high, flip_low):
    count = flip_high.shape[1]
    whole = pl.BlockSpec((count, W), lambda i, r: (0, 0))
    block = [pl.BlockSpec((BLK, count), functools.partial(lambda j, i, r: (r[4 * i + j], 0), j)) for j in range(4)]
    return pl.pallas_call(
        near_kernel,
        grid_spec=pltpu.PrefetchScalarGridSpec(
            num_scalar_prefetch=1,
            grid=(3,),
            in_specs=block + block + [whole, whole],
            out_specs=pl.BlockSpec((1, 4 * BLK, W), lambda i, r: (i, 0, 0)),
        ),
        out_shape=jax.ShapeDtypeStruct((3, 4 * BLK, W), F32),
        compiler_params=params(),
        name="near",
    )(rows, *([flip_high] * 4), *([flip_low] * 4), panel_high, panel_low)


def col_ring(s):
    return [(i, (i + 2 * s) % 8) for i in range(8)]


def row_ring(over, s):
    if over == "z":
        return [(r, (r + 4 * s) % 16) for r in range(16)]
    return [(r, r // 4 * 4 + (r + s) % 4) for r in range(16)]


def gather_row(panel, first):
    mine = [panel] + [lax.ppermute(panel, "col", col_ring(s)) for s in (1, 3, 2)]
    mine, first = lax.optimization_barrier((mine, first))
    return mine + [lax.ppermute(piece, "col", SWAP) for piece in mine], first


def gather_places(x, k):
    places = []
    for core in (k, 1 - k):
        places += [((x + 4 - s) % 4) * 2 + core for s in (0, 1, 3, 2)]
    return jnp.stack(places).astype(jnp.int32)


def block_at(z, y, x, k):
    moved = (y // 2 + k) % 2
    upper = moved * (1 - y % 2) + (1 - moved) * (y % 2)
    return upper * 8 + (z + x) % 4 * 2 + moved


def chunk_rows(over, place, x, k):
    if over == "z":
        return [block_at(place, j, x, k) for j in range(4)]
    return [block_at(j, place, x, k) for j in range(4)]


def home_pairs():
    pairs = []
    for z in range(4):
        for y in range(4):
            for x in range(4):
                for k in range(2):
                    col = 2 * x + k
                    pairs.append(((z * 4 + y) * 8 + col, col * 16 + block_at(z, y, x, k)))
    return pairs


def sweep(pieces, places, over, place, other, x, k, flip_high, flip_low):
    chunk = lambda s: chunk_rows(over, (place + s) % 4, x, k)
    table = lambda rows: jnp.stack(rows).astype(jnp.int32)
    high, low, top, bottom = far_product(table(chunk(2)), places, pieces, flip_high, flip_low)
    top = lax.ppermute(top, "row", row_ring(over, 1))
    bottom = lax.ppermute(bottom, "row", row_ring(over, 3))
    near = near_product(table(chunk(1) + chunk(3) + chunk(0)), high, low, flip_high, flip_low)
    ahead = jnp.concatenate([near[0, : 2 * BLK] + top, near[0, 2 * BLK :]], axis=0)
    behind = jnp.concatenate([near[1, : 2 * BLK], near[1, 2 * BLK :] + bottom], axis=0)
    ahead = lax.ppermute(ahead, "row", row_ring(over, 1))
    behind = lax.ppermute(behind, "row", row_ring(over, 3))
    total = (near[2] + (ahead + behind)).reshape(4, BLK, W)
    across = "y" if over == "z" else "z"
    pick = lambda s: lax.dynamic_index_in_dim(total, (other + s) % 4, 0, keepdims=False)
    return pick(0) + sum(lax.ppermute(pick(s), "row", row_ring(across, s)) for s in (1, 2, 3))


def sum_over_all(part, k, beside):
    rows = part.shape[0]
    split = part.reshape(2, rows // 2, BLK)
    keep = lax.dynamic_index_in_dim(split, k, 0, keepdims=False)
    give = lax.dynamic_index_in_dim(split, 1 - k, 0, keepdims=False)
    kept = keep + lax.ppermute(give, "col", SWAP)
    piece = rows // 32
    mine = lax.all_to_all(kept.reshape(16, piece, BLK), "row", 0, 0, tiled=True).sum(axis=0)
    mine = mine + sum(lax.ppermute(mine, "col", col_ring(s)) for s in (1, 2, 3))
    mine, beside = lax.optimization_barrier((mine, beside))
    wide = jnp.broadcast_to(mine[None], (16, piece, BLK))
    half = lax.all_to_all(wide, "row", 0, 0, tiled=True).reshape(rows // 2, BLK)
    return half, lax.ppermute(half, "col", SWAP), beside


def finish_kernel(core, half, other, square_one, square_top, base_two, one, cross, two, total):
    rows = half.shape[0]
    k = core[0]
    total[pl.ds(pl.multiple_of(k * rows, 8), rows), :] = half[...]
    total[pl.ds(pl.multiple_of((1 - k) * rows, 8), rows), :] = other[...]
    at = 0
    for out, base in ((one, square_one), (cross, square_top), (two, base_two)):
        for j in range(4):
            cols = slice(j * BLK, (j + 1) * BLK)
            if out is cross:
                out[:, cols] = total[at : at + W, :] - base[:, cols]
                at += W
                continue
            size = W - j * BLK
            out[j * BLK :, cols] = total[at : at + size, :] + base[j * BLK :, cols]
            for i in range(j + 1, 4):
                below = total[at + (i - j) * BLK : at + (i - j + 1) * BLK, :]
                rows_i = slice(i * BLK, (i + 1) * BLK)
                out[cols, rows_i] = below.T + base[cols, rows_i]
            at += size


def finish(k, half, other, square_one, square_top, base_two):
    square = jax.ShapeDtypeStruct((W, W), F32)
    vmem = pl.BlockSpec(memory_space=pltpu.VMEM)
    return pl.pallas_call(
        finish_kernel,
        in_specs=[pl.BlockSpec(memory_space=pltpu.SMEM)] + [vmem] * 5,
        out_specs=[vmem] * 3,
        out_shape=[square] * 3,
        scratch_shapes=[pltpu.VMEM((2 * half.shape[0], BLK), F32)],
        compiler_params=params(),
        name="finish",
    )(k.reshape(1).astype(jnp.int32), half, other, square_one, square_top, base_two)


def body(
    trailing,
    factor_one,
    inverse_one,
    factor_two_top,
    factor_two,
    inverse_two,
    structure_one,
    structure_two,
):
    row = lax.axis_index("row")
    col = lax.axis_index("col")
    z, y, x, k = row // 4, row % 4, col // 2, col % 2
    mask_one = block_flag(structure_one, row * 8 + col)
    mask_two = block_flag(structure_two, row * 8 + col)
    places = gather_places(x, k)
    home_way = home_pairs()
    out_way = [(there, here) for here, there in home_way]

    normal_one = mask_one * product(factor_one, inverse_one)
    flips = flipped(trailing)
    pieces_one, flips = gather_row(normal_one, flips)
    flip_high, flip_low = flips
    normal_top = product(factor_two_top, inverse_two)
    panel_two = mask_two * product(factor_two, inverse_two) - product(normal_one, normal_top)
    moved_one = lax.ppermute(normal_one, BOTH, out_way)
    moved_two = lax.ppermute(panel_two, BOTH, out_way)
    pieces_two, moved_one = gather_row(panel_two, moved_one)

    sums_one = sweep(pieces_one, places, "z", z, y, x, k, flip_high, flip_low)
    pieces_two, moved_two = lax.optimization_barrier((pieces_two, moved_two))
    sums_two = sweep(pieces_two, places, "y", y, z, x, k, flip_high, flip_low)
    sums = jnp.concatenate([sums_one, sums_two], axis=1)

    panels = jnp.concatenate([moved_one, moved_two], axis=1)
    quad = product_t(panels, sums)
    cut = lambda first, last, j: quad[first:last, j * BLK : (j + 1) * BLK]
    parts = [cut(j * BLK, W, j) for j in range(4)]
    parts += [cut(0, W, 4 + j) for j in range(4)]
    parts += [cut(W + j * BLK, 2 * W, 4 + j) for j in range(4)]
    home = lax.ppermute(sums, BOTH, home_way)
    half, other, home = sum_over_all(jnp.concatenate(parts, axis=0), k, home)
    column_one = -mask_one * home[:, :W]
    column_two = -mask_two * home[:, W:]
    square_one = product_t(inverse_one, inverse_one)
    square_top = product(square_one, normal_top)
    base_two = product_t(inverse_two, inverse_two) + product_t(normal_top, square_top)
    diagonal_one, cross_two, diagonal_two = finish(k, half, other, square_one, square_top, base_two)
    return (column_one, diagonal_one, column_two, cross_two, diagonal_two)


def solution(mesh):
    return jax.shard_map(
        body,
        mesh=mesh,
        in_specs=(
            P("row", "col"),
            P(("row", "col"), None),
            P(),
            P(),
            P(("row", "col"), None),
            P(),
            P(),
            P(),
        ),
        out_specs=(P(("row", "col"), None), P(), P(("row", "col"), None), P(), P()),
        check_vma=False,
    )
```

```python
import functools

import jax
import jax.numpy as jnp
from jax import lax
from jax.experimental import pallas as pl
from jax.experimental.pallas import tpu as pltpu
from jax.sharding import PartitionSpec as P

BLK = 128
W = 512
BOTH = ("row", "col")
SWAP = [(i, i ^ 1) for i in range(8)]
F32 = jnp.float32
BF16 = jnp.bfloat16


def product(left, right):
    return jnp.dot(left, right, precision=lax.Precision.HIGH, preferred_element_type=F32)


def product_t(left, right):
    return lax.dot_general(
        left, right, (((0,), (0,)), ((), ())), precision=lax.Precision.HIGH, preferred_element_type=F32
    )


def block_flag(structure, block):
    return jnp.any(structure == block).astype(F32)


def params(mib):
    return pltpu.CompilerParams(vmem_limit_bytes=mib << 20)


def pinned(value, space=pltpu.HBM):
    return pltpu.with_memory_space_constraint(value, space)


def halves(value):
    high = value.astype(BF16)
    return high, (value - high.astype(F32)).astype(BF16)


def three(left_high, left_low, right_high, right_low):
    dot = functools.partial(jnp.dot, preferred_element_type=F32)
    return dot(left_high, right_high) + (dot(left_low, right_high) + dot(left_high, right_low))


def flip_kernel(blocks, left, right, high, low):
    for i, block in enumerate((left, right)):
        high[0, i], low[0, i] = halves(block[...].T)


def flipped(trailing, blocks):
    rows = trailing.shape[0]
    out = pltpu.HBM((4, 4, BLK, rows), BF16)
    spec = pl.BlockSpec((1, 2, BLK, rows), lambda i, b: (i // 2, i % 2, 0, 0))
    return pl.pallas_call(
        flip_kernel,
        grid_spec=pltpu.PrefetchScalarGridSpec(
            num_scalar_prefetch=1,
            grid=(8,),
            in_specs=[
                pl.BlockSpec((rows, BLK), lambda i, b: (0, b[2 * i])),
                pl.BlockSpec((rows, BLK), lambda i, b: (0, b[2 * i + 1])),
            ],
            out_specs=[spec, spec],
        ),
        out_shape=[out, out],
        compiler_params=params(12),
        name="flip",
    )(blocks, trailing, trailing)


def far_kernel(chunks, places, *refs):
    pieces, (flip_high, flip_low), (high, low, top, bottom) = refs[:8], refs[8:10], refs[10:]
    for i in range(8):
        at = pl.ds(pl.multiple_of(places[i] * BLK, BLK), BLK)
        high[at, :], low[at, :] = halves(pieces[i][...])
    out = chunk_product(flip_high, flip_low, high, low)
    top[...] = out[: 2 * BLK]
    bottom[...] = out[2 * BLK :]


def chunk_product(flip_high, flip_low, high, low):
    shape = (4 * BLK, flip_high.shape[-1])
    return three(flip_high[...].reshape(shape), flip_low[...].reshape(shape), high[...], low[...])


def near_kernel(chunks, flip_high, flip_low, high, low, *outs):
    for s in range(3):

        @pl.when(pl.program_id(0) == s)
        def _():
            outs[s][...] = chunk_product(flip_high, flip_low, high, low)


def flip_specs(over, count):
    if over == "z":
        return [pl.BlockSpec((1, 4, BLK, count), lambda i, c, *p: (c[i], 0, 0, 0))] * 2
    return [pl.BlockSpec((4, 1, BLK, count), lambda i, c, *p: (0, c[i], 0, 0))] * 2


def whole(shape):
    return pl.BlockSpec(shape, lambda i, *p: (0, 0))


def far_product(which, chunks, places, pieces, flip_high, flip_low):
    count = flip_high.shape[-1]
    return pl.pallas_call(
        far_kernel,
        grid_spec=pltpu.PrefetchScalarGridSpec(
            num_scalar_prefetch=2,
            grid=(1,),
            in_specs=[pl.BlockSpec((BLK, W), lambda i, *p: (0, which))] * 8 + flip_specs("zy"[which], count),
            out_specs=[whole((count, W))] * 2 + [whole((2 * BLK, W))] * 2,
        ),
        out_shape=[pltpu.HBM((count, W), BF16)] * 2 + [jax.ShapeDtypeStruct((2 * BLK, W), F32)] * 2,
        compiler_params=params(22),
        name="far",
    )(chunks, places, *pieces, pinned(flip_high), pinned(flip_low))


def near_product(which, chunks, panel_high, panel_low, flip_high, flip_low):
    count = flip_high.shape[-1]
    return pl.pallas_call(
        near_kernel,
        grid_spec=pltpu.PrefetchScalarGridSpec(
            num_scalar_prefetch=1,
            grid=(3,),
            in_specs=flip_specs("zy"[which], count) + [whole((count, W))] * 2,
            out_specs=[whole((4 * BLK, W))] * 3,
        ),
        out_shape=[jax.ShapeDtypeStruct((4 * BLK, W), F32)] * 3,
        compiler_params=params(22),
        name="near",
    )(chunks, pinned(flip_high), pinned(flip_low), pinned(panel_high), pinned(panel_low))


def join_kernel(ahead, behind, top, bottom, ahead_out, behind_out):
    ahead_out[...] = ahead[...] + top[...]
    behind_out[...] = behind[...] + bottom[...]


def join(ahead, behind, top, bottom):
    half = (2 * BLK, W)
    upper, lower = pl.BlockSpec(half, lambda i: (0, 0)), pl.BlockSpec(half, lambda i: (1, 0))
    return pl.pallas_call(
        join_kernel,
        grid=(1,),
        in_specs=[upper, lower, upper, upper],
        out_specs=[upper, lower],
        out_shape=[jax.ShapeDtypeStruct(ahead.shape, F32)] * 2,
        input_output_aliases={0: 0, 1: 1},
        compiler_params=params(10),
        name="join",
    )(ahead, behind, top, bottom)


def fold_kernel(place, own, one, other, *refs):
    outs, total = refs[:4], refs[4]
    total[...] = own[...] + (one[...] + other[...])
    for s, out in enumerate(outs):
        out[...] = total[pl.ds(pl.multiple_of((place[0] + s) % 4 * BLK, BLK), BLK), :]


def fold(place, *chunks):
    vmem = pl.BlockSpec(memory_space=pltpu.VMEM)
    return pl.pallas_call(
        fold_kernel,
        in_specs=[pl.BlockSpec(memory_space=pltpu.SMEM)] + [vmem] * 3,
        out_specs=[vmem] * 4,
        out_shape=[jax.ShapeDtypeStruct((BLK, W), F32)] * 4,
        scratch_shapes=[pltpu.VMEM((4 * BLK, W), F32)],
        compiler_params=params(10),
        name="fold",
    )(place.reshape(1).astype(jnp.int32), *chunks)


def col_ring(s):
    return [(i, (i + 2 * s) % 8) for i in range(8)]


def row_ring(over, s):
    if over == "z":
        return [(r, (r + 4 * s) % 16) for r in range(16)]
    return [(r, r // 4 * 4 + (r + s) % 4) for r in range(16)]


def gather_row(panel):
    return [panel] + [lax.ppermute(panel, "col", col_ring(s)) for s in (1, 3, 2)]


def gather_places(x, k):
    places = []
    for core in (k, 1 - k):
        places += [((x + 4 - s) % 4) * 2 + core for s in (0, 1, 3, 2)]
    return jnp.stack(places).astype(jnp.int32)


def block_at(z, y, x, k):
    moved = (y // 2 + k) % 2
    upper = moved * (1 - y % 2) + (1 - moved) * (y % 2)
    return upper * 8 + (z + x) % 4 * 2 + moved


def home_pairs():
    pairs = []
    for z in range(4):
        for y in range(4):
            for x in range(4):
                for k in range(2):
                    col = 2 * x + k
                    pairs.append(((z * 4 + y) * 8 + col, col * 16 + block_at(z, y, x, k)))
    return pairs


def table(rows):
    return jnp.stack(rows).astype(jnp.int32)


def strip_kernel(col, part, high_one, low_one, high_two, low_two, out, whole_strip):
    rows = part.shape[0] * BLK
    right_high, right_low = halves(part[...].reshape(rows, BLK))
    for i, (high, low) in enumerate(((high_one, low_one), (high_two, low_two))):
        dot = lambda left, right: lax.dot_general(left, right, (((0,), (0,)), ((), ())), preferred_element_type=F32)
        total = dot(low[...], right_high) + dot(high[...], right_low)
        whole_strip[i * W : (i + 1) * W] = dot(high[...], right_high) + total
    for i in range(5):
        at = pl.multiple_of((col[0] + i) % 8 * BLK, BLK)
        out[i * BLK : (i + 1) * BLK] = whole_strip[pl.ds(at, BLK)]


def strip(col, part, panels):
    vmem = pl.BlockSpec(memory_space=pltpu.VMEM)
    return pl.pallas_call(
        strip_kernel,
        in_specs=[pl.BlockSpec(memory_space=pltpu.SMEM)] + [vmem] * 5,
        out_specs=vmem,
        out_shape=jax.ShapeDtypeStruct((5 * BLK, BLK), F32),
        scratch_shapes=[pltpu.VMEM((8 * BLK, BLK), F32)],
        compiler_params=params(16),
        name="strip",
    )(col.reshape(1).astype(jnp.int32), part, *panels)


def sum_over_rows(part):
    piece = part.shape[0] // 16
    mine = lax.all_to_all(part.reshape(16, piece, BLK), "row", 0, 0, tiled=True).sum(axis=0)
    wide = jnp.broadcast_to(mine[None], (16, piece, BLK))
    return lax.all_to_all(wide, "row", 0, 0, tiled=True).reshape(part.shape)


def finish_kernel(places, *refs):
    strips, (square_one, square_top, base_two), (one, cross, two), total = refs[:8], refs[8:11], refs[11:14], refs[14]
    rows = 5 * BLK
    for i, piece in enumerate(strips):
        total[pl.ds(pl.multiple_of(places[i] * rows, BLK), rows), :] = piece[...]

    def block(r, q):
        if (r - q) % 8 <= 4:
            at = q * rows + (r - q) % 8 * BLK
            return total[at : at + BLK, :]
        at = r * rows + (q - r) % 8 * BLK
        return total[at : at + BLK, :].T

    for i in range(4):
        for j in range(4):
            at = (slice(i * BLK, (i + 1) * BLK), slice(j * BLK, (j + 1) * BLK))
            one[at] = square_one[at] + block(i, j)
            cross[at] = block(i, 4 + j) - square_top[at]
            two[at] = base_two[at] + block(4 + i, 4 + j)


def finish(places, strips, bases):
    square = jax.ShapeDtypeStruct((W, W), F32)
    vmem = pl.BlockSpec(memory_space=pltpu.VMEM)
    return pl.pallas_call(
        finish_kernel,
        in_specs=[pl.BlockSpec(memory_space=pltpu.SMEM)] + [vmem] * 11,
        out_specs=[vmem] * 3,
        out_shape=[square] * 3,
        scratch_shapes=[pltpu.VMEM((8 * 5 * BLK, BLK), F32)],
        compiler_params=params(16),
        name="finish",
    )(places, *strips, *bases)


def body(
    trailing,
    factor_one,
    inverse_one,
    factor_two_top,
    factor_two,
    inverse_two,
    structure_one,
    structure_two,
):
    row = lax.axis_index("row")
    col = lax.axis_index("col")
    z, y, x, k = row // 4, row % 4, col // 2, col % 2
    mask_one = block_flag(structure_one, row * 8 + col)
    mask_two = block_flag(structure_two, row * 8 + col)
    places = gather_places(x, k)
    home_way = home_pairs()

    normal_one = mask_one * product(factor_one, inverse_one)
    normal_top = product(factor_two_top, inverse_two)
    panel_two = mask_two * product(factor_two, inverse_two) - product(normal_one, normal_top)
    pieces = gather_row(jnp.concatenate([normal_one, panel_two], axis=1))
    trailing, pieces[0] = lax.optimization_barrier((trailing, pieces[0]))
    flips = flipped(trailing, table([block_at(i // 4, i % 4, x, k) for i in range(16)]))
    pieces, flips = lax.optimization_barrier((pieces, flips))
    pieces += [lax.ppermute(piece, "col", SWAP) for piece in pieces]

    def forward(over):
        return lambda value: lax.ppermute(value, "row", row_ring(over, 1))

    def backward(over):
        return lambda value: lax.ppermute(value, "row", row_ring(over, 3))

    def chunks(place, shifts):
        return table([(place + s) % 4 for s in shifts])

    def light(across, picks):
        return picks[0] + sum(lax.ppermute(picks[s], "row", row_ring(across, s)) for s in (1, 2, 3))

    order = lax.optimization_barrier
    high, low, top_one, bottom_one = far_product(0, chunks(z, [2]), places, pieces, *flips)
    panels = [high, low]
    top_one, bottom_one = forward("z")(top_one), backward("z")(bottom_one)
    high, low, top_two, bottom_two = far_product(1, chunks(y, [2]), places, pieces, *flips)
    panels += [high, low]
    top_two, bottom_two = forward("y")(top_two), backward("y")(bottom_two)
    ahead, behind, own_one = near_product(0, chunks(z, [1, 3, 0]), *panels[:2], *flips)
    ahead, behind = join(ahead, behind, top_one, bottom_one)
    rest_one = (forward("z")(ahead), backward("z")(behind))
    ahead, behind, own_two = near_product(1, chunks(y, [1, 3, 0]), *panels[2:], *flips)
    ahead, behind = join(ahead, behind, top_two, bottom_two)
    rest_two = (forward("y")(ahead), backward("y")(behind))
    own_one, own_two = order((own_one, own_two))

    sums_one = lax.ppermute(light("y", fold(y, own_one, *rest_one)), BOTH, home_way)
    sums_two = lax.ppermute(light("z", fold(z, own_two, *rest_two)), BOTH, home_way)
    column_one = -mask_one * sums_one
    column_two = -mask_two * sums_two

    square_one = product_t(inverse_one, inverse_one)
    square_top = product(square_one, normal_top)
    base_two = product_t(inverse_two, inverse_two) + product_t(normal_top, square_top)
    cut = lambda sums, j: sums[:, j * BLK : (j + 1) * BLK]
    part = jnp.stack([cut(sums, j) for sums in (sums_one, sums_two) for j in range(4)])
    part = lax.all_to_all(part, "col", 0, 0, tiled=True)
    total = sum_over_rows(strip(col, part, panels))
    strips = [total] + [lax.ppermute(total, "col", col_ring(s)) for s in (1, 3, 2)]
    strips += [lax.ppermute(piece, "col", SWAP) for piece in strips]
    diagonal_one, cross_two, diagonal_two = finish(places, strips, (square_one, square_top, base_two))
    return (column_one, diagonal_one, column_two, cross_two, diagonal_two)


def solution(mesh):
    return jax.shard_map(
        body,
        mesh=mesh,
        in_specs=(
            P("row", "col"),
            P(("row", "col"), None),
            P(),
            P(),
            P(("row", "col"), None),
            P(),
            P(),
            P(),
        ),
        out_specs=(P(("row", "col"), None), P(), P(("row", "col"), None), P(), P()),
        check_vma=False,
    )
```

```python
import functools

import jax
import jax.numpy as jnp
from jax import lax
from jax.experimental import pallas as pl
from jax.experimental.pallas import tpu as pltpu
from jax.sharding import PartitionSpec as P

BLK = 128
W = 512
BOTH = ("row", "col")
SWAP = [(i, i ^ 1) for i in range(8)]
F32 = jnp.float32
BF16 = jnp.bfloat16


def product(left, right):
    return jnp.dot(left, right, precision=lax.Precision.HIGH, preferred_element_type=F32)


def product_t(left, right):
    return lax.dot_general(
        left, right, (((0,), (0,)), ((), ())), precision=lax.Precision.HIGH, preferred_element_type=F32
    )


def block_flag(structure, block):
    return jnp.any(structure == block).astype(F32)


def params(mib):
    return pltpu.CompilerParams(vmem_limit_bytes=mib << 20)


def pinned(value, space=pltpu.HBM):
    return pltpu.with_memory_space_constraint(value, space)


def halves(value):
    high = value.astype(BF16)
    return high, (value - high.astype(F32)).astype(BF16)


def three(left_high, left_low, right_high, right_low):
    dot = functools.partial(jnp.dot, preferred_element_type=F32)
    return dot(left_high, right_high) + (dot(left_low, right_high) + dot(left_high, right_low))


def flip_kernel(blocks, left, right, high, low):
    for i, block in enumerate((left, right)):
        high[0, i], low[0, i] = halves(block[...].T)


def flipped(trailing, blocks):
    rows = trailing.shape[0]
    out = pltpu.HBM((4, 4, BLK, rows), BF16)
    spec = pl.BlockSpec((1, 2, BLK, rows), lambda i, b: (i // 2, i % 2, 0, 0))
    return pl.pallas_call(
        flip_kernel,
        grid_spec=pltpu.PrefetchScalarGridSpec(
            num_scalar_prefetch=1,
            grid=(8,),
            in_specs=[
                pl.BlockSpec((rows, BLK), lambda i, b: (0, b[2 * i])),
                pl.BlockSpec((rows, BLK), lambda i, b: (0, b[2 * i + 1])),
            ],
            out_specs=[spec, spec],
        ),
        out_shape=[out, out],
        compiler_params=params(12),
        name="flip",
    )(blocks, trailing, trailing)


def far_kernel(chunks, places, *refs):
    pieces, (flip_high, flip_low), (high, low, top, bottom) = refs[:8], refs[8:10], refs[10:]
    for i in range(8):
        at = pl.ds(pl.multiple_of(places[i] * BLK, BLK), BLK)
        high[at, :], low[at, :] = halves(pieces[i][...])
    out = chunk_product(flip_high, flip_low, high, low)
    top[...] = out[: 2 * BLK]
    bottom[...] = out[2 * BLK :]


def chunk_product(flip_high, flip_low, high, low):
    shape = (4 * BLK, flip_high.shape[-1])
    return three(flip_high[...].reshape(shape), flip_low[...].reshape(shape), high[...], low[...])


def near_kernel(chunks, flip_high, flip_low, high, low, *outs):
    for s in range(len(outs)):

        @pl.when(pl.program_id(0) == s)
        def _():
            outs[s][...] = chunk_product(flip_high, flip_low, high, low)


def flip_specs(over, count):
    if over == "z":
        return [pl.BlockSpec((1, 4, BLK, count), lambda i, c, *p: (c[i], 0, 0, 0))] * 2
    return [pl.BlockSpec((4, 1, BLK, count), lambda i, c, *p: (0, c[i], 0, 0))] * 2


def whole(shape):
    return pl.BlockSpec(shape, lambda i, *p: (0, 0))


def far_product(which, chunks, places, pieces, flip_high, flip_low):
    count = flip_high.shape[-1]
    return pl.pallas_call(
        far_kernel,
        grid_spec=pltpu.PrefetchScalarGridSpec(
            num_scalar_prefetch=2,
            grid=(1,),
            in_specs=[whole((BLK, W))] * 8 + flip_specs("zy"[which], count),
            out_specs=[whole((count, W))] * 2 + [whole((2 * BLK, W))] * 2,
        ),
        out_shape=[pltpu.HBM((count, W), BF16)] * 2 + [jax.ShapeDtypeStruct((2 * BLK, W), F32)] * 2,
        compiler_params=params(22),
        name="far",
    )(chunks, places, *pieces, pinned(flip_high), pinned(flip_low))


def near_product(which, chunks, panel_high, panel_low, flip_high, flip_low):
    count, number = flip_high.shape[-1], chunks.shape[0]
    return pl.pallas_call(
        near_kernel,
        grid_spec=pltpu.PrefetchScalarGridSpec(
            num_scalar_prefetch=1,
            grid=(number,),
            in_specs=flip_specs("zy"[which], count) + [whole((count, W))] * 2,
            out_specs=[whole((4 * BLK, W))] * number,
        ),
        out_shape=[jax.ShapeDtypeStruct((4 * BLK, W), F32)] * number,
        compiler_params=params(22),
        name="near",
    )(chunks, pinned(flip_high), pinned(flip_low), pinned(panel_high), pinned(panel_low))


def join_kernel(ahead, behind, top, bottom, ahead_out, behind_out):
    ahead_out[...] = ahead[...] + top[...]
    behind_out[...] = behind[...] + bottom[...]


def join(ahead, behind, top, bottom):
    half = (2 * BLK, W)
    upper, lower = pl.BlockSpec(half, lambda i: (0, 0)), pl.BlockSpec(half, lambda i: (1, 0))
    return pl.pallas_call(
        join_kernel,
        grid=(1,),
        in_specs=[upper, lower, upper, upper],
        out_specs=[upper, lower],
        out_shape=[jax.ShapeDtypeStruct(ahead.shape, F32)] * 2,
        input_output_aliases={0: 0, 1: 1},
        compiler_params=params(10),
        name="join",
    )(ahead, behind, top, bottom)


def fold_kernel(place, own, one, other, *refs):
    outs, total = refs[:4], refs[4]
    total[...] = own[...] + (one[...] + other[...])
    for s, out in enumerate(outs):
        out[...] = total[pl.ds(pl.multiple_of((place[0] + s) % 4 * BLK, BLK), BLK), :]


def fold(place, *chunks):
    vmem = pl.BlockSpec(memory_space=pltpu.VMEM)
    return pl.pallas_call(
        fold_kernel,
        in_specs=[pl.BlockSpec(memory_space=pltpu.SMEM)] + [vmem] * 3,
        out_specs=[vmem] * 4,
        out_shape=[jax.ShapeDtypeStruct((BLK, W), F32)] * 4,
        scratch_shapes=[pltpu.VMEM((4 * BLK, W), F32)],
        compiler_params=params(10),
        name="fold",
    )(place.reshape(1).astype(jnp.int32), *chunks)


def col_ring(s):
    return [(i, (i + 2 * s) % 8) for i in range(8)]


def row_ring(over, s):
    if over == "z":
        return [(r, (r + 4 * s) % 16) for r in range(16)]
    return [(r, r // 4 * 4 + (r + s) % 4) for r in range(16)]


def gather_row(panel):
    return [panel] + [lax.ppermute(panel, "col", col_ring(s)) for s in (1, 3, 2)]


def gather_places(x, k):
    places = []
    for core in (k, 1 - k):
        places += [((x + 4 - s) % 4) * 2 + core for s in (0, 1, 3, 2)]
    return jnp.stack(places).astype(jnp.int32)


def block_at(z, y, x, k):
    moved = (y // 2 + k) % 2
    upper = moved * (1 - y % 2) + (1 - moved) * (y % 2)
    return upper * 8 + (z + x) % 4 * 2 + moved


def home_pairs():
    pairs = []
    for z in range(4):
        for y in range(4):
            for x in range(4):
                for k in range(2):
                    col = 2 * x + k
                    pairs.append(((z * 4 + y) * 8 + col, col * 16 + block_at(z, y, x, k)))
    return pairs


def table(rows):
    return jnp.stack(rows).astype(jnp.int32)


def strip_kernel(col, part, high_one, low_one, high_two, low_two, out, whole_strip):
    rows = part.shape[0] * BLK
    right_high, right_low = halves(part[...].reshape(rows, BLK))
    for i, (high, low) in enumerate(((high_one, low_one), (high_two, low_two))):
        dot = lambda left, right: lax.dot_general(left, right, (((0,), (0,)), ((), ())), preferred_element_type=F32)
        total = dot(low[...], right_high) + dot(high[...], right_low)
        whole_strip[i * W : (i + 1) * W] = dot(high[...], right_high) + total
    for i in range(5):
        at = pl.multiple_of((col[0] + i) % 8 * BLK, BLK)
        out[i * BLK : (i + 1) * BLK] = whole_strip[pl.ds(at, BLK)]


def strip(col, part, panels):
    vmem = pl.BlockSpec(memory_space=pltpu.VMEM)
    return pl.pallas_call(
        strip_kernel,
        in_specs=[pl.BlockSpec(memory_space=pltpu.SMEM)] + [vmem] * 5,
        out_specs=vmem,
        out_shape=jax.ShapeDtypeStruct((5 * BLK, BLK), F32),
        scratch_shapes=[pltpu.VMEM((8 * BLK, BLK), F32)],
        compiler_params=params(16),
        name="strip",
    )(col.reshape(1).astype(jnp.int32), part, *panels)


def sum_over_rows(part):
    piece = part.shape[0] // 16
    mine = lax.all_to_all(part.reshape(16, piece, BLK), "row", 0, 0, tiled=True).sum(axis=0)
    wide = jnp.broadcast_to(mine[None], (16, piece, BLK))
    return lax.all_to_all(wide, "row", 0, 0, tiled=True).reshape(part.shape)


def finish_kernel(places, *refs):
    strips, (square_one, square_top, base_two), (one, cross, two), total = refs[:8], refs[8:11], refs[11:14], refs[14]
    rows = 5 * BLK
    for i, piece in enumerate(strips):
        total[pl.ds(pl.multiple_of(places[i] * rows, BLK), rows), :] = piece[...]

    def block(r, q):
        if (r - q) % 8 <= 4:
            at = q * rows + (r - q) % 8 * BLK
            return total[at : at + BLK, :]
        at = r * rows + (q - r) % 8 * BLK
        return total[at : at + BLK, :].T

    for i in range(4):
        for j in range(4):
            at = (slice(i * BLK, (i + 1) * BLK), slice(j * BLK, (j + 1) * BLK))
            one[at] = square_one[at] + block(i, j)
            cross[at] = block(i, 4 + j) - square_top[at]
            two[at] = base_two[at] + block(4 + i, 4 + j)


def finish(places, strips, bases):
    square = jax.ShapeDtypeStruct((W, W), F32)
    vmem = pl.BlockSpec(memory_space=pltpu.VMEM)
    return pl.pallas_call(
        finish_kernel,
        in_specs=[pl.BlockSpec(memory_space=pltpu.SMEM)] + [vmem] * 11,
        out_specs=[vmem] * 3,
        out_shape=[square] * 3,
        scratch_shapes=[pltpu.VMEM((8 * 5 * BLK, BLK), F32)],
        compiler_params=params(16),
        name="finish",
    )(places, *strips, *bases)


def body(
    trailing,
    factor_one,
    inverse_one,
    factor_two_top,
    factor_two,
    inverse_two,
    structure_one,
    structure_two,
):
    row = lax.axis_index("row")
    col = lax.axis_index("col")
    z, y, x, k = row // 4, row % 4, col // 2, col % 2
    mask_one = block_flag(structure_one, row * 8 + col)
    mask_two = block_flag(structure_two, row * 8 + col)
    places = gather_places(x, k)
    home_way = home_pairs()

    normal_one = mask_one * product(factor_one, inverse_one)
    pieces_one = gather_row(normal_one)
    normal_top = product(factor_two_top, inverse_two)
    panel_two = mask_two * product(factor_two, inverse_two) - product(normal_one, normal_top)
    pieces_two = gather_row(panel_two)
    order = lax.optimization_barrier
    trailing, pieces_one[0] = order((trailing, pieces_one[0]))
    flips = flipped(trailing, table([block_at(i // 4, i % 4, x, k) for i in range(16)]))
    pieces_one, flips = order((pieces_one, flips))
    pieces_one += [lax.ppermute(piece, "col", SWAP) for piece in pieces_one]

    def forward(over):
        return lambda value: lax.ppermute(value, "row", row_ring(over, 1))

    def backward(over):
        return lambda value: lax.ppermute(value, "row", row_ring(over, 3))

    def chunks(place, shifts):
        return table([(place + s) % 4 for s in shifts])

    def light(across, picks):
        return picks[0] + sum(lax.ppermute(picks[s], "row", row_ring(across, s)) for s in (1, 2, 3))

    high, low, top_one, bottom_one = far_product(0, chunks(z, [2]), places, pieces_one, *flips)
    top_one, bottom_one = forward("z")(top_one), backward("z")(bottom_one)
    panels = [high, low]
    panels[0], pieces_two = order((panels[0], pieces_two))
    pieces_two += [lax.ppermute(piece, "col", SWAP) for piece in pieces_two]
    high, low, top_two, bottom_two = far_product(1, chunks(y, [2]), places, pieces_two, *flips)
    panels += [high, low]
    top_two, bottom_two = forward("y")(top_two), backward("y")(bottom_two)
    ahead_two, behind_two = near_product(1, chunks(y, [1, 3]), *panels[2:], *flips)
    panels[0], ahead_two = order((panels[0], ahead_two))
    ahead, behind = near_product(0, chunks(z, [1, 3]), *panels[:2], *flips)
    ahead_two, behind_two = join(ahead_two, behind_two, top_two, bottom_two)
    rest_two = (forward("y")(ahead_two), backward("y")(behind_two))
    ahead, behind = join(ahead, behind, top_one, bottom_one)
    ahead, panels[1], panels[3] = order((ahead, panels[1], panels[3]))
    rest_one = (forward("z")(ahead), backward("z")(behind))
    (own_one,) = near_product(0, chunks(z, [0]), *panels[:2], *flips)
    (own_two,) = near_product(1, chunks(y, [0]), *panels[2:], *flips)

    own_one, own_two = order((own_one, own_two))

    sums_one = lax.ppermute(light("y", fold(y, own_one, *rest_one)), BOTH, home_way)
    sums_two = lax.ppermute(light("z", fold(z, own_two, *rest_two)), BOTH, home_way)
    column_one = -mask_one * sums_one
    column_two = -mask_two * sums_two

    square_one = product_t(inverse_one, inverse_one)
    square_top = product(square_one, normal_top)
    base_two = product_t(inverse_two, inverse_two) + product_t(normal_top, square_top)
    cut = lambda sums, j: sums[:, j * BLK : (j + 1) * BLK]
    part = jnp.stack([cut(sums, j) for sums in (sums_one, sums_two) for j in range(4)])
    part = lax.all_to_all(part, "col", 0, 0, tiled=True)
    total = sum_over_rows(strip(col, part, panels))
    strips = [total] + [lax.ppermute(total, "col", col_ring(s)) for s in (1, 3, 2)]
    strips += [lax.ppermute(piece, "col", SWAP) for piece in strips]
    diagonal_one, cross_two, diagonal_two = finish(places, strips, (square_one, square_top, base_two))
    return (column_one, diagonal_one, column_two, cross_two, diagonal_two)


def solution(mesh):
    return jax.shard_map(
        body,
        mesh=mesh,
        in_specs=(
            P("row", "col"),
            P(("row", "col"), None),
            P(),
            P(),
            P(("row", "col"), None),
            P(),
            P(),
            P(),
        ),
        out_specs=(P(("row", "col"), None), P(), P(("row", "col"), None), P(), P()),
        check_vma=False,
    )
```

```python
import functools

import jax
import jax.numpy as jnp
from jax import lax
from jax.experimental import pallas as pl
from jax.experimental.pallas import tpu as pltpu
from jax.sharding import PartitionSpec as P

BLK = 128
W = 512
BOTH = ("row", "col")
SWAP = [(i, i ^ 1) for i in range(8)]
F32 = jnp.float32
BF16 = jnp.bfloat16


def product(left, right):
    return jnp.dot(left, right, precision=lax.Precision.HIGH, preferred_element_type=F32)


def product_t(left, right):
    return lax.dot_general(
        left, right, (((0,), (0,)), ((), ())), precision=lax.Precision.HIGH, preferred_element_type=F32
    )


def block_flag(structure, block):
    return jnp.any(structure == block).astype(F32)


def params(mib):
    return pltpu.CompilerParams(vmem_limit_bytes=mib << 20)


def pinned(value, space=pltpu.HBM):
    return pltpu.with_memory_space_constraint(value, space)


def halves(value):
    high = value.astype(BF16)
    return high, (value - high.astype(F32)).astype(BF16)


def three(left_high, left_low, right_high, right_low):
    dot = functools.partial(jnp.dot, preferred_element_type=F32)
    return dot(left_high, right_high) + (dot(left_low, right_high) + dot(left_high, right_low))


def flip_kernel(blocks, left, right, high, low):
    for i, block in enumerate((left, right)):
        high[0, i], low[0, i] = halves(block[...].T)


def flipped(trailing, blocks):
    rows = trailing.shape[0]
    out = pltpu.HBM((4, 4, BLK, rows), BF16)
    spec = pl.BlockSpec((1, 2, BLK, rows), lambda i, b: (i // 2, i % 2, 0, 0))
    return pl.pallas_call(
        flip_kernel,
        grid_spec=pltpu.PrefetchScalarGridSpec(
            num_scalar_prefetch=1,
            grid=(8,),
            in_specs=[
                pl.BlockSpec((rows, BLK), lambda i, b: (0, b[2 * i])),
                pl.BlockSpec((rows, BLK), lambda i, b: (0, b[2 * i + 1])),
            ],
            out_specs=[spec, spec],
        ),
        out_shape=[out, out],
        compiler_params=params(12),
        name="flip",
    )(blocks, trailing, trailing)


def far_kernel(chunks, places, *refs):
    pieces, (flip_high, flip_low), (high, low, top, bottom) = refs[:8], refs[8:10], refs[10:]
    for i in range(8):
        at = pl.ds(pl.multiple_of(places[i] * BLK, BLK), BLK)
        high[at, :], low[at, :] = halves(pieces[i][...])
    out = chunk_product(flip_high, flip_low, high, low)
    top[...] = out[: 2 * BLK]
    bottom[...] = out[2 * BLK :]


def chunk_product(flip_high, flip_low, high, low):
    shape = (4 * BLK, flip_high.shape[-1])
    return three(flip_high[...].reshape(shape), flip_low[...].reshape(shape), high[...], low[...])


def near_kernel(chunks, flip_high, flip_low, high, low, *outs):
    for s in range(len(outs)):

        @pl.when(pl.program_id(0) == s)
        def _():
            outs[s][...] = chunk_product(flip_high, flip_low, high, low)


def flip_specs(over, count):
    if over == "z":
        return [pl.BlockSpec((1, 4, BLK, count), lambda i, c, *p: (c[i], 0, 0, 0))] * 2
    return [pl.BlockSpec((4, 1, BLK, count), lambda i, c, *p: (0, c[i], 0, 0))] * 2


def whole(shape):
    return pl.BlockSpec(shape, lambda i, *p: (0, 0))


def far_product(which, chunks, places, pieces, flip_high, flip_low):
    count = flip_high.shape[-1]
    return pl.pallas_call(
        far_kernel,
        grid_spec=pltpu.PrefetchScalarGridSpec(
            num_scalar_prefetch=2,
            grid=(1,),
            in_specs=[whole((BLK, W))] * 8 + flip_specs("zy"[which], count),
            out_specs=[whole((count, W))] * 2 + [whole((2 * BLK, W))] * 2,
        ),
        out_shape=[pltpu.HBM((count, W), BF16)] * 2 + [jax.ShapeDtypeStruct((2 * BLK, W), F32)] * 2,
        compiler_params=params(22),
        name="far",
    )(chunks, places, *pieces, pinned(flip_high), pinned(flip_low))


def near_product(which, chunks, panel_high, panel_low, flip_high, flip_low):
    count, number = flip_high.shape[-1], chunks.shape[0]
    return pl.pallas_call(
        near_kernel,
        grid_spec=pltpu.PrefetchScalarGridSpec(
            num_scalar_prefetch=1,
            grid=(number,),
            in_specs=flip_specs("zy"[which], count) + [whole((count, W))] * 2,
            out_specs=[whole((4 * BLK, W))] * number,
        ),
        out_shape=[jax.ShapeDtypeStruct((4 * BLK, W), F32)] * number,
        compiler_params=params(22),
        name="near",
    )(chunks, pinned(flip_high), pinned(flip_low), pinned(panel_high), pinned(panel_low))


def join_kernel(ahead, behind, top, bottom, ahead_out, behind_out):
    ahead_out[...] = ahead[...] + top[...]
    behind_out[...] = behind[...] + bottom[...]


def join(ahead, behind, top, bottom):
    half = (2 * BLK, W)
    upper, lower = pl.BlockSpec(half, lambda i: (0, 0)), pl.BlockSpec(half, lambda i: (1, 0))
    return pl.pallas_call(
        join_kernel,
        grid=(1,),
        in_specs=[upper, lower, upper, upper],
        out_specs=[upper, lower],
        out_shape=[jax.ShapeDtypeStruct(ahead.shape, F32)] * 2,
        input_output_aliases={0: 0, 1: 1},
        compiler_params=params(10),
        name="join",
    )(ahead, behind, top, bottom)


def fold_kernel(place, own, one, other, *refs):
    outs, total = refs[:4], refs[4]
    total[...] = own[...] + (one[...] + other[...])
    for s, out in enumerate(outs):
        out[...] = total[pl.ds(pl.multiple_of((place[0] + s) % 4 * BLK, BLK), BLK), :]


def fold(place, *chunks):
    vmem = pl.BlockSpec(memory_space=pltpu.VMEM)
    return pl.pallas_call(
        fold_kernel,
        in_specs=[pl.BlockSpec(memory_space=pltpu.SMEM)] + [vmem] * 3,
        out_specs=[vmem] * 4,
        out_shape=[jax.ShapeDtypeStruct((BLK, W), F32)] * 4,
        scratch_shapes=[pltpu.VMEM((4 * BLK, W), F32)],
        compiler_params=params(10),
        name="fold",
    )(place.reshape(1).astype(jnp.int32), *chunks)


def col_ring(s):
    return [(i, (i + 2 * s) % 8) for i in range(8)]


def row_ring(over, s):
    if over == "z":
        return [(r, (r + 4 * s) % 16) for r in range(16)]
    return [(r, r // 4 * 4 + (r + s) % 4) for r in range(16)]


def gather_row(panel):
    return [panel] + [lax.ppermute(panel, "col", col_ring(s)) for s in (1, 3, 2)]


def gather_places(x, k):
    places = []
    for core in (k, 1 - k):
        places += [((x + 4 - s) % 4) * 2 + core for s in (0, 1, 3, 2)]
    return jnp.stack(places).astype(jnp.int32)


def block_at(z, y, x, k):
    moved = (y // 2 + k) % 2
    upper = moved * (1 - y % 2) + (1 - moved) * (y % 2)
    return upper * 8 + (z + x) % 4 * 2 + moved


def home_pairs():
    pairs = []
    for z in range(4):
        for y in range(4):
            for x in range(4):
                for k in range(2):
                    col = 2 * x + k
                    pairs.append(((z * 4 + y) * 8 + col, col * 16 + block_at(z, y, x, k)))
    return pairs


def table(rows):
    return jnp.stack(rows).astype(jnp.int32)


def strip_kernel(col, part, high_one, low_one, high_two, low_two, out, whole_strip):
    rows = part.shape[0] * BLK
    right_high, right_low = halves(part[...].reshape(rows, BLK))
    for i, (high, low) in enumerate(((high_one, low_one), (high_two, low_two))):
        dot = lambda left, right: lax.dot_general(left, right, (((0,), (0,)), ((), ())), preferred_element_type=F32)
        total = dot(low[...], right_high) + dot(high[...], right_low)
        whole_strip[i * W : (i + 1) * W] = dot(high[...], right_high) + total
    for i in range(5):
        at = pl.multiple_of((col[0] + i) % 8 * BLK, BLK)
        out[i * BLK : (i + 1) * BLK] = whole_strip[pl.ds(at, BLK)]


def strip(col, part, panels):
    vmem = pl.BlockSpec(memory_space=pltpu.VMEM)
    return pl.pallas_call(
        strip_kernel,
        in_specs=[pl.BlockSpec(memory_space=pltpu.SMEM)] + [vmem] * 5,
        out_specs=vmem,
        out_shape=jax.ShapeDtypeStruct((5 * BLK, BLK), F32),
        scratch_shapes=[pltpu.VMEM((8 * BLK, BLK), F32)],
        compiler_params=params(16),
        name="strip",
    )(col.reshape(1).astype(jnp.int32), part, *panels)


def sum_over_rows(part):
    piece = part.shape[0] // 16
    mine = lax.all_to_all(part.reshape(16, piece, BLK), "row", 0, 0, tiled=True).sum(axis=0)
    wide = jnp.broadcast_to(mine[None], (16, piece, BLK))
    return lax.all_to_all(wide, "row", 0, 0, tiled=True).reshape(part.shape)


def finish_kernel(places, *refs):
    strips, (square_one, square_top, base_two), (one, cross, two), total = refs[:8], refs[8:11], refs[11:14], refs[14]
    rows = 5 * BLK
    for i, piece in enumerate(strips):
        total[pl.ds(pl.multiple_of(places[i] * rows, BLK), rows), :] = piece[...]

    def block(r, q):
        if (r - q) % 8 <= 4:
            at = q * rows + (r - q) % 8 * BLK
            return total[at : at + BLK, :]
        at = r * rows + (q - r) % 8 * BLK
        return total[at : at + BLK, :].T

    for i in range(4):
        for j in range(4):
            at = (slice(i * BLK, (i + 1) * BLK), slice(j * BLK, (j + 1) * BLK))
            one[at] = square_one[at] + block(i, j)
            cross[at] = block(i, 4 + j) - square_top[at]
            two[at] = base_two[at] + block(4 + i, 4 + j)


def finish(places, strips, bases):
    square = jax.ShapeDtypeStruct((W, W), F32)
    vmem = pl.BlockSpec(memory_space=pltpu.VMEM)
    return pl.pallas_call(
        finish_kernel,
        in_specs=[pl.BlockSpec(memory_space=pltpu.SMEM)] + [vmem] * 11,
        out_specs=[vmem] * 3,
        out_shape=[square] * 3,
        scratch_shapes=[pltpu.VMEM((8 * 5 * BLK, BLK), F32)],
        compiler_params=params(16),
        name="finish",
    )(places, *strips, *bases)


def body(
    trailing,
    factor_one,
    inverse_one,
    factor_two_top,
    factor_two,
    inverse_two,
    structure_one,
    structure_two,
):
    row = lax.axis_index("row")
    col = lax.axis_index("col")
    z, y, x, k = row // 4, row % 4, col // 2, col % 2
    mask_one = block_flag(structure_one, row * 8 + col)
    mask_two = block_flag(structure_two, row * 8 + col)
    places = gather_places(x, k)
    home_way = home_pairs()

    normal_one = mask_one * product(factor_one, inverse_one)
    pieces_one = gather_row(normal_one)
    normal_top = product(factor_two_top, inverse_two)
    panel_two = mask_two * product(factor_two, inverse_two) - product(normal_one, normal_top)
    pieces_two = gather_row(panel_two)
    order = lax.optimization_barrier
    trailing, pieces_one[0] = order((trailing, pieces_one[0]))
    flips = flipped(trailing, table([block_at(i // 4, i % 4, x, k) for i in range(16)]))
    pieces_one, flips = order((pieces_one, flips))
    pieces_one += [lax.ppermute(piece, "col", SWAP) for piece in pieces_one]

    def forward(over):
        return lambda value: lax.ppermute(value, "row", row_ring(over, 1))

    def backward(over):
        return lambda value: lax.ppermute(value, "row", row_ring(over, 3))

    def chunks(place, shifts):
        return table([(place + s) % 4 for s in shifts])

    def light(across, picks):
        return picks[0] + sum(lax.ppermute(picks[s], "row", row_ring(across, s)) for s in (1, 2, 3))

    high, low, top_one, bottom_one = far_product(0, chunks(z, [2]), places, pieces_one, *flips)
    top_one, bottom_one = forward("z")(top_one), backward("z")(bottom_one)
    panels = [high, low]
    ahead, behind = near_product(0, chunks(z, [1, 3]), *panels[:2], *flips)
    behind, pieces_two = order((behind, pieces_two))
    pieces_two += [lax.ppermute(piece, "col", SWAP) for piece in pieces_two]
    high, low, top_two, bottom_two = far_product(1, chunks(y, [2]), places, pieces_two, *flips)
    panels += [high, low]
    top_two, bottom_two = forward("y")(top_two), backward("y")(bottom_two)
    ahead_two, behind_two = near_product(1, chunks(y, [1, 3]), *panels[2:], *flips)
    ahead_two, behind_two = join(ahead_two, behind_two, top_two, bottom_two)
    rest_two = (forward("y")(ahead_two), backward("y")(behind_two))
    ahead, behind = join(ahead, behind, top_one, bottom_one)
    ahead, ahead_two, panels[1], panels[3] = order((ahead, ahead_two, panels[1], panels[3]))
    rest_one = (forward("z")(ahead), backward("z")(behind))
    (own_one,) = near_product(0, chunks(z, [0]), *panels[:2], *flips)
    (own_two,) = near_product(1, chunks(y, [0]), *panels[2:], *flips)

    own_one, own_two = order((own_one, own_two))

    sums_one = lax.ppermute(light("y", fold(y, own_one, *rest_one)), BOTH, home_way)
    sums_two = lax.ppermute(light("z", fold(z, own_two, *rest_two)), BOTH, home_way)
    column_one = -mask_one * sums_one
    column_two = -mask_two * sums_two

    square_one = product_t(inverse_one, inverse_one)
    square_top = product(square_one, normal_top)
    base_two = product_t(inverse_two, inverse_two) + product_t(normal_top, square_top)
    cut = lambda sums, j: sums[:, j * BLK : (j + 1) * BLK]
    part = jnp.stack([cut(sums, j) for sums in (sums_one, sums_two) for j in range(4)])
    part = lax.all_to_all(part, "col", 0, 0, tiled=True)
    total = sum_over_rows(strip(col, part, panels))
    strips = [total] + [lax.ppermute(total, "col", col_ring(s)) for s in (1, 3, 2)]
    strips += [lax.ppermute(piece, "col", SWAP) for piece in strips]
    diagonal_one, cross_two, diagonal_two = finish(places, strips, (square_one, square_top, base_two))
    return (column_one, diagonal_one, column_two, cross_two, diagonal_two)


def solution(mesh):
    return jax.shard_map(
        body,
        mesh=mesh,
        in_specs=(
            P("row", "col"),
            P(("row", "col"), None),
            P(),
            P(),
            P(("row", "col"), None),
            P(),
            P(),
            P(),
        ),
        out_specs=(P(("row", "col"), None), P(), P(("row", "col"), None), P(), P()),
        check_vma=False,
    )
```
